32 devices in a mesh: dp: 4 (over z), ctx: 4 (over y, x), tensor: 2 (over core).
Axes of the slice: x: 2, y: 2, z: 4, core: 2. Of those that a mesh axis runs over, the one named last changes fastest.
Arguments:
- layer_input: bfloat16 [4, 2, 1024, 2048], P('dp', None, 'ctx'), may hold values from -6 to 6
- out_grad: bfloat16 [4, 2, 1024, 2048], P('dp', None, 'ctx'), may hold values from -6 to 6
- seq_count: int32 [4], P('dp'), may hold values from 1 to 2, as said below
- seq_order: int32 [4, 2], P('dp'), may hold values from 0 to 1, each once within a row
- ln1_gain: float32 [2048], replicated, may hold values from 0.5 to 1.5
- ln1_bias: float32 [2048], replicated, may hold values from -1 to 1
- ln2_gain: float32 [2048], replicated, may hold values from 0.5 to 1.5
- ln2_bias: float32 [2048], replicated, may hold values from -1 to 1
- w_qkv: bfloat16 [2048, 3, 8, 256], P('ctx', None, 'tensor'), may hold values from -0.125 to 0.125
- b_qkv: float32 [3, 8, 256], P(None, 'tensor'), may hold values from -3 to 3
- w_out: bfloat16 [8, 256, 2048], P('tensor', None, 'ctx'), may hold values from -3 to 3
- b_out: float32 [2048], replicated, may hold values from -2 to 2
- w_up: bfloat16 [2048, 8192], P('ctx', 'tensor'), may hold values from -0.125 to 0.125
- b_up: float32 [8192], P('tensor'), may hold values from -3 to 3
- w_down: bfloat16 [8192, 2048], P('tensor', 'ctx'), may hold values from -0.0625 to 0.0625
- b_down: float32 [2048], replicated, may hold values from -2 to 2
Outputs:
- layer_output: bfloat16 [4, 2, 1024, 2048], P('dp', None, 'ctx')
- x_grad: bfloat16 [4, 2, 1024, 2048], P('dp', None, 'ctx')
- g_ln1_gain: float32 [2048], replicated
- g_ln1_bias: float32 [2048], replicated
- g_ln2_gain: float32 [2048], replicated
- g_ln2_bias: float32 [2048], replicated
- g_w_qkv: float32 [2048, 3, 8, 256], P(('dp', 'ctx'), None, 'tensor')
- g_b_qkv: float32 [3, 8, 256], P(None, 'tensor')
- g_w_out: float32 [8, 256, 2048], P('tensor', None, ('dp', 'ctx'))
- g_b_out: float32 [2048], replicated
- g_w_up: float32 [2048, 8192], P(('dp', 'ctx'), 'tensor')
- g_b_up: float32 [8192], P('tensor')
- g_w_down: float32 [8192, 2048], P('tensor', ('dp', 'ctx'))
- g_b_down: float32 [2048], replicated
The draws below stay inside these ranges and needn't reach their ends.
Inputs may be any that keep to these rules, and one draw needn't show every extreme that they name: `seq_count`: live sequence slots of each replica; in every draw some replica has 2 and another has 1. Each row is a permutation of the 2 slots; replica r's live slots are seq_order[r, j] for j < seq_count[r].
All inputs are finite; a program needn't handle non-finite values.
Results may differ from the reference program's by a relative error of at most 0.011.
Values may be sent and summed in bfloat16 or wider, within the bound.
No kernel may reach another device: no remote copies, remote signals or barrier semaphores. Data moves between devices by JAX's collectives and lax.ppermute only.
A program may use at most 384 MiB of HBM per device.

```python
import math
import jax
import jax.numpy as jnp
from jax import lax

D = 2048
HEADS = 8
HD = 256
FF = 8192
ROT = 64
BLK = 256
MB = 2
SEQ = 1024
REPLICAS = 4


def draw_seq_count(key, part):
    first, second = jax.random.split(key, 2)
    counts = jax.random.randint(first, (REPLICAS,), 1, MB + 1)
    order = jax.random.permutation(second, REPLICAS)
    spots = jnp.arange(REPLICAS, dtype=jnp.int32)
    counts = jnp.where(spots == order[0], MB, counts)
    counts = jnp.where(spots == order[1], 1, counts)
    return counts.astype(jnp.int32)


def steps_of(key, extent, shards, smallest, largest):
    level, own = 1.0, jax.random.fold_in(key, 6)
    for position, shards_of in shards:
        steps = jnp.exp(jax.random.uniform(jax.random.fold_in(own, position), (shards_of,), jnp.float32, smallest / len(shards), largest / len(shards)))
        level = level * jnp.repeat(steps, extent[position] // shards_of).reshape([-1 if axis == position else 1 for axis in range(len(extent))])
    return level


def normal_values(own_key, dims, width, bound, shards=(), kind=jnp.bfloat16):
    factor_of = steps_of(own_key, dims, shards, -0.22, 0.18) if shards else 1.0
    values = jax.random.normal(own_key, dims, jnp.float32) * width * factor_of
    return jnp.minimum(jnp.maximum(values, -bound), bound).astype(kind)


def setup_inputs(seed: int = 0) -> dict:
    key_list = jax.random.split(jax.random.key(seed), 17)
    return {
        "layer_input": normal_values(key_list[0], (REPLICAS, MB, SEQ, D), 1.0, 6.0, ((0, 4), (2, 4))),
        "out_grad": normal_values(key_list[1], (REPLICAS, MB, SEQ, D), 1.0, 6.0, ((0, 4), (2, 4))),
        "seq_count": draw_seq_count(jax.random.fold_in(key_list[16], 71), 0),
        "seq_order": jax.vmap(lambda own: jax.random.permutation(own, MB))(jax.random.split(key_list[3], REPLICAS)).reshape((REPLICAS, MB)).astype(jnp.int32),
        "ln1_gain": jnp.clip(1.0 + 0.1 * jax.random.normal(key_list[4], (D,), jnp.float32), 0.5, 1.5),
        "ln1_bias": normal_values(key_list[5], (D,), 0.2, 1.0, (), jnp.float32),
        "ln2_gain": jnp.clip(1.0 + 0.1 * jax.random.normal(key_list[6], (D,), jnp.float32), 0.5, 1.5),
        "ln2_bias": normal_values(key_list[7], (D,), 0.2, 1.0, (), jnp.float32),
        "w_qkv": normal_values(key_list[8], (D, 3, HEADS, HD), D ** -0.5, 0.125, ((0, 4), (2, 2))),
        "b_qkv": normal_values(key_list[9], (3, HEADS, HD), 0.5, 3.0, ((1, 2),), jnp.float32),
        "w_out": normal_values(key_list[10], (HEADS, HD, D), (max(D // 512, 1)) ** -0.5, 3.0, ((0, 2), (2, 4))),
        "b_out": normal_values(key_list[11], (D,), 0.3, 2.0, (), jnp.float32),
        "w_up": normal_values(key_list[12], (D, FF), D ** -0.5, 0.125, ((0, 4), (1, 2))),
        "b_up": normal_values(key_list[13], (FF,), 0.5, 3.0, ((0, 2),), jnp.float32),
        "w_down": normal_values(key_list[14], (FF, D), FF ** -0.5, 0.0625, ((0, 2), (1, 4))),
        "b_down": normal_values(key_list[15], (D,), 0.3, 2.0, (), jnp.float32),
    }


@jax.custom_vjp
def low(v):
    return lax.optimization_barrier(v.astype(jnp.bfloat16)).astype(jnp.float32)

@jax.custom_vjp
def low_back(v):
    return v

def low_keep(v):
    return (low(v), None)

def low_pass(kept, grad):
    return (grad,)

def back_keep(v):
    return (v, None)

def back_low(kept, grad):
    return (low(grad),)
low.defvjp(low_keep, low_pass)
low_back.defvjp(back_keep, back_low)
norm_eps = 1e-05
masked_value = -1e+30
highest = lax.Precision.HIGHEST

def layer_norm(values, gain, shift):
    centre = values - lax.optimization_barrier(jnp.mean(values, -1, keepdims=True))
    spread = lax.optimization_barrier(jnp.mean(centre * centre, -1, keepdims=True))
    return centre * lax.rsqrt(spread + norm_eps) * gain + shift

def rotate(values, positions):
    half_rot = ROT // 2
    freqs = jnp.exp(jnp.arange(half_rot, dtype=jnp.float32) * (-2.0 * math.log(10000.0) / ROT))
    angles = positions[:, None].astype(jnp.float32) * freqs[None, :]
    angles = jnp.concatenate([angles, angles], -1)
    cosine = jnp.cos(angles)[:, None, :]
    sine = jnp.sin(angles)[:, None, :]
    rotary = values[..., :ROT]
    turned = jnp.concatenate([-rotary[..., half_rot:], rotary[..., :half_rot]], -1)
    return jnp.concatenate([rotary * cosine + turned * sine, values[..., ROT:]], -1)

def forward(params, seq_in):
    gain_one, bias_one, gain_two, bias_two, qkv_weight, qkv_bias, out_weight, out_bias, up_weight, up_bias, down_weight, down_bias = params
    positions = jnp.arange(SEQ, dtype=jnp.int32)
    blocks = positions // BLK
    allowed = blocks[None, :] <= blocks[:, None]
    normed_one = low(layer_norm(seq_in, gain_one, bias_one))
    normed_two = low(layer_norm(seq_in, gain_two, bias_two))
    projected = low_back(jnp.einsum('td,dshe->tshe', normed_one, qkv_weight, precision=highest) + qkv_bias)
    queries = low(rotate(projected[:, 0], positions))
    keys_rot = low(rotate(projected[:, 1], positions))
    values_in = low(projected[:, 2])
    score_scale = 1.0 / math.sqrt(HD)
    scores = low_back(jnp.einsum('qhe,khe->hqk', queries, keys_rot, precision=highest) * score_scale)
    masked = jnp.where(allowed[None], scores, masked_value)
    expo = jnp.exp(masked - lax.optimization_barrier(jnp.max(masked, -1, keepdims=True)))
    probs = expo / lax.optimization_barrier(jnp.sum(expo, -1, keepdims=True))
    attended = low(low_back(jnp.einsum('hqk,khe->qhe', low(probs), values_in, precision=highest)))
    attn_part = jnp.einsum('qhe,hed->qd', attended, out_weight, precision=highest)
    up_pre = low_back(jnp.dot(normed_two, up_weight, precision=highest) + up_bias)
    acted = low(jax.nn.gelu(up_pre, approximate=False))
    mlp_part = jnp.dot(acted, down_weight, precision=highest)
    return seq_in + attn_part + mlp_part + out_bias + down_bias

def reference(layer_input, out_grad, seq_count, seq_order, ln1_gain, ln1_bias, ln2_gain, ln2_bias, w_qkv, b_qkv, w_out, b_out, w_up, b_up, w_down, b_down):
    slots = jnp.arange(MB, dtype=jnp.int32)
    taken = (seq_order[:, :, None] == slots[None, None, :]) & (slots[None, :, None] < seq_count[:, None, None])
    live = jnp.any(taken, axis=1).astype(jnp.float32).reshape(REPLICAS * MB)
    inputs = layer_input.astype(jnp.float32).reshape(REPLICAS * MB, SEQ, D)
    cotangents = out_grad.astype(jnp.float32).reshape(REPLICAS * MB, SEQ, D) * live[:, None, None]
    params = tuple((item.astype(jnp.float32) for item in (ln1_gain, ln1_bias, ln2_gain, ln2_bias, w_qkv, b_qkv, w_out, b_out, w_up, b_up, w_down, b_down)))
    zeros = tuple((jnp.zeros_like(item) for item in params))

    def one_sequence(totals, item):
        seq_in, seq_cot = item
        outputs, pull = jax.vjp(forward, params, seq_in)
        grad_params, grad_in = pull(seq_cot)
        return (tuple((left + right for left, right in zip(totals, grad_params))), (outputs, grad_in))
    totals, (outputs, grad_in) = lax.scan(one_sequence, zeros, (inputs, cotangents))
    outputs = (outputs * live[:, None, None]).reshape(REPLICAS, MB, SEQ, D).astype(jnp.bfloat16)
    grad_in = grad_in.reshape(REPLICAS, MB, SEQ, D).astype(jnp.bfloat16)
    return (outputs, grad_in, totals[0], totals[1], totals[2], totals[3], totals[4], totals[5], totals[6], totals[7], totals[8], totals[9], totals[10], totals[11])
```

```python
import functools
import math

import jax
import jax.numpy as jnp
from jax import lax
from jax.experimental import pallas as pl
from jax.experimental.pallas import tpu as pltpu
from jax.sharding import PartitionSpec as P

ROT = 64


norm_eps = 1e-05
masked_value = -1e30
low = jnp.bfloat16
full = jnp.float32


def swap(value, axis, size, step):
    return lax.ppermute(value, axis, [(i, i ^ step) for i in range(size)])


def dot(left, right, dims):
    return lax.dot_general(left, right, (dims, ((), ())), preferred_element_type=full)


def rotary_tables(positions, lanes):
    half_rot = ROT // 2
    freqs = jnp.exp(jnp.arange(half_rot, dtype=full) * (-2.0 * math.log(10000.0) / ROT))
    angles = positions[:, None].astype(full) * freqs[None, :]
    cosine, sine = jnp.cos(angles), jnp.sin(angles)
    rest = (positions.shape[0], lanes - ROT)
    return (
        jnp.concatenate([cosine, cosine, jnp.ones(rest, full)], -1),
        jnp.concatenate([-sine, sine, jnp.zeros(rest, full)], -1),
    )


def attention_kernel(
    ctx_ref, qkv_ref, do_ref, cos_ref, sin_ref, o_ref, dqkv_ref, q_s, k_s, v_s, do_s, dk_s, dv_s
):
    parts, blocks, _, rows, width = qkv_ref.shape
    head = width // 3
    lanes = cos_ref.shape[-1]
    size = parts * rows
    ctx = ctx_ref[0]
    lane = lax.broadcasted_iota(jnp.int32, (rows, lanes), 1)
    first = lane < ROT // 2

    def turn(values, cosine, sine):
        part = values[:, :lanes]
        swapped = jnp.where(
            first, pltpu.roll(part, lanes - ROT // 2, 1), pltpu.roll(part, ROT // 2, 1)
        )
        return jnp.concatenate([part * cosine + swapped * sine, values[:, lanes:]], -1)

    dk_s[...] = jnp.zeros_like(dk_s)
    dv_s[...] = jnp.zeros_like(dv_s)
    for block in range(blocks):
        place = jnp.bitwise_xor(ctx, block)
        for part in range(parts):
            at = slice(block * size + part * rows, block * size + (part + 1) * rows)
            values = qkv_ref[part, place, 0]
            cosine, sine = cos_ref[part, place], sin_ref[part, place]
            q_s[at, :] = turn(values[:, :head], cosine, sine).astype(low)
            k_s[at, :] = turn(values[:, head : 2 * head], cosine, sine).astype(low)
            v_s[at, :] = values[:, 2 * head :].astype(low)
            do_s[at, :] = do_ref[part, place, 0]
    scale = 1.0 / math.sqrt(head)
    for block in range(blocks):
        place = jnp.bitwise_xor(ctx, block)
        own = slice(block * size, (block + 1) * size)
        seen = slice(0, (block + 1) * size)
        q, do = q_s[own, :], do_s[own, :]
        k, v = k_s[seen, :], v_s[seen, :]
        scores = dot(q, k, ((1,), (1,))) * scale
        expo = jnp.exp(scores - jnp.max(scores, -1, keepdims=True))
        probs = expo / jnp.sum(expo, -1, keepdims=True)
        probs_low = probs.astype(low)
        attended = dot(probs_low, v, ((1,), (0,))).astype(low)
        grad_probs = dot(do, v, ((1,), (1,)))
        grad_scores = (
            probs * (grad_probs - jnp.sum(probs * grad_probs, -1, keepdims=True))
        ).astype(low)
        dq = dot(grad_scores, k, ((1,), (0,))) * scale
        dk_s[seen, :] += dot(grad_scores, q, ((0,), (0,))) * scale
        dv_s[seen, :] += dot(probs_low, do, ((0,), (0,)))
        for part in range(parts):
            at = slice(part * rows, (part + 1) * rows)
            cosine, sine = cos_ref[part, place], sin_ref[part, place]
            o_ref[part, place, 0] = attended[at]
            dqkv_ref[part, place, 0, :, :head] = turn(dq[at], cosine, -sine).astype(low)
    for block in range(blocks):
        place = jnp.bitwise_xor(ctx, block)
        for part in range(parts):
            at = slice(block * size + part * rows, block * size + (part + 1) * rows)
            cosine, sine = cos_ref[part, place], sin_ref[part, place]
            dqkv_ref[part, place, 0, :, head : 2 * head] = turn(
                dk_s[at, :], cosine, -sine
            ).astype(low)
            dqkv_ref[part, place, 0, :, 2 * head :] = dv_s[at, :].astype(low)


def attention(ctx_index, qkv, grad_o, cosine, sine):
    parts, blocks, slots, rows, width = qkv.shape
    head, lanes = width // 3, cosine.shape[-1]
    total = parts * blocks * rows

    def piece(last):
        return pl.BlockSpec((parts, blocks, 1, rows, last), lambda s, c: (0, 0, s, 0, 0))

    table = pl.BlockSpec((parts, blocks, rows, lanes), lambda s, c: (0, 0, 0, 0))
    return pl.pallas_call(
        attention_kernel,
        out_shape=(
            jax.ShapeDtypeStruct((parts, blocks, slots, rows, head), low),
            jax.ShapeDtypeStruct((parts, blocks, slots, rows, width), low),
        ),
        grid_spec=pltpu.PrefetchScalarGridSpec(
            num_scalar_prefetch=1,
            grid=(slots,),
            in_specs=[piece(width), piece(head), table, table],
            out_specs=(piece(head), piece(width)),
            scratch_shapes=[pltpu.VMEM((total, head), low)] * 4
            + [pltpu.VMEM((total, head), full)] * 2,
        ),
        compiler_params=pltpu.CompilerParams(vmem_limit_bytes=48 << 20),
        name="attention",
    )(ctx_index[None], qkv, grad_o, cosine, sine)


def normalize(values):
    centre = values - jnp.mean(values, -1, keepdims=True)
    spread = jnp.mean(centre * centre, -1, keepdims=True)
    return centre * lax.rsqrt(spread + norm_eps)


def gelu_both(values):
    cumulative = 0.5 * (1.0 + lax.erf(values * math.sqrt(0.5)))
    density = jnp.exp(-0.5 * values * values) * (1.0 / math.sqrt(2.0 * math.pi))
    return values * cumulative, cumulative + values * density


def split_body(
    layer_input,
    out_grad,
    seq_count,
    seq_order,
    ln1_gain,
    ln1_bias,
    ln2_gain,
    ln2_bias,
    w_qkv,
    b_qkv,
    w_out,
    b_out,
    w_up,
    b_up,
    w_down,
    b_down,
):
    ctx, cores, reps = lax.axis_size("ctx"), lax.axis_size("tensor"), lax.axis_size("dp")
    _, slots, block_len, width = layer_input.shape
    here, core = lax.axis_index("ctx"), lax.axis_index("tensor")
    rows = block_len // cores
    tokens = ctx * slots * block_len
    heads = w_qkv.shape[2] // ctx
    head = w_qkv.shape[3]
    hidden = w_up.shape[1] // ctx

    def across(value, step):
        return swap(value, "ctx", ctx, step)

    def partner(value):
        return swap(value, "tensor", cores, 1)

    def exchange(value, split, join):
        each = value.shape[split] // ctx
        shape = list(value.shape)
        shape[split] = each
        step = shape[join]
        shape[join] *= ctx
        result = jnp.zeros(shape, value.dtype)
        for k in range(ctx):
            peer = jnp.bitwise_xor(here, k)
            piece = lax.dynamic_slice_in_dim(value, peer * each, each, split)
            piece = across(piece, k) if k else piece
            result = lax.dynamic_update_slice_in_dim(result, piece, peer * step, join)
        return result

    def gather(own):
        first, second = across(own, 1), across(own, 2)
        third = jnp.concatenate([across(first[:1], 2), across(second[1:], 1)], 0)
        return jnp.stack([own, first, second, third])

    def scatter(parts):
        by_two = across(parts[3, :1].astype(low), 2)
        by_one = across(parts[3, 1:].astype(low), 1)
        first = jnp.concatenate([parts[1, :1] + by_two.astype(full), parts[1, 1:]], 0)
        second = jnp.concatenate([parts[2, :1], parts[2, 1:] + by_one.astype(full)], 0)
        first, second = across(first.astype(low), 1), across(second.astype(low), 2)
        return parts[0] + first.astype(full) + second.astype(full)

    def whole_replica(value):
        own = lax.dynamic_slice_in_dim(value, core * rows, rows, 1)
        other = lax.dynamic_slice_in_dim(value, (1 - core) * rows, rows, 1)
        mine = gather(own)
        theirs = jnp.concatenate([other[None], partner(mine[1:])], 0)
        return jnp.stack([mine, theirs])

    def own_rows(partial):
        parts = partial[0].astype(full) + partner(partial[1].astype(low)).astype(full)
        return scatter(parts)

    def both_cores(mine):
        theirs = partner(mine)
        low_rows = jnp.where(core == 0, mine, theirs)
        high_rows = jnp.where(core == 0, theirs, mine)
        return jnp.concatenate([low_rows, high_rows], 1)[None]

    turns = jnp.arange(slots, dtype=jnp.int32)
    taken = (seq_order[0][:, None] == turns[None, :]) & (turns[:, None] < seq_count[0])
    live = jnp.any(taken, axis=0).astype(full)[:, None, None]
    inputs = layer_input[0]
    cots = (out_grad[0].astype(full) * live).astype(low)

    x_all = whole_replica(inputs).reshape(tokens, width)
    up_w = exchange(w_up, 1, 0)
    g_all = whole_replica(cots).reshape(tokens, width)
    down_w = exchange(w_down, 0, 1)
    qkv_w = exchange(w_qkv, 2, 0).reshape(width, 3 * heads * head)
    out_w = exchange(w_out, 0, 2).reshape(heads * head, width)

    unit = normalize(x_all.astype(full))
    normed_one = (unit * ln1_gain + ln1_bias).astype(low)
    normed_two = (unit * ln2_gain + ln2_bias).astype(low)

    up_bias = lax.dynamic_slice_in_dim(b_up, here * hidden, hidden, 0)
    up_pre = dot(normed_two, up_w, ((1,), (0,))) + up_bias
    acted, slope = gelu_both(up_pre)
    acted = acted.astype(low)
    grad_up = (dot(g_all, down_w, ((1,), (1,))) * slope).astype(low)

    qkv_bias = lax.dynamic_slice_in_dim(b_qkv, here * heads, heads, 1).reshape(-1)
    qkv = dot(normed_one, qkv_w, ((1,), (0,))) + qkv_bias
    grad_o = dot(g_all, out_w, ((1,), (1,))).astype(low)
    order = jnp.arange(cores * ctx * rows, dtype=jnp.int32)
    part, block, row = order // (ctx * rows), order // rows % ctx, order % rows
    positions = (here ^ block) * block_len + (part ^ core) * rows + row
    lanes = min(head, 128)
    cosine, sine = (
        table.reshape(cores, ctx, rows, lanes) for table in rotary_tables(positions, lanes)
    )
    grouped = (cores, ctx, slots, rows)
    attended, grad_qkv = attention(
        here,
        qkv.reshape(*grouped, 3 * head),
        grad_o.reshape(*grouped, head),
        cosine,
        sine,
    )
    attended = attended.reshape(tokens, head)
    grad_qkv = grad_qkv.reshape(tokens, 3 * head)

    partial_out = dot(attended, out_w, ((1,), (0,))) + dot(acted, down_w, ((1,), (0,)))
    branch = own_rows(partial_out.reshape(*grouped, width))
    own_x = lax.dynamic_slice_in_dim(inputs, core * rows, rows, 1).astype(full)
    own_g = lax.dynamic_slice_in_dim(cots, core * rows, rows, 1).astype(full)
    out_rows = both_cores(((own_x + branch + b_out + b_down) * live).astype(low))

    partial_unit = (
        dot(grad_qkv, qkv_w, ((1,), (1,))) * ln1_gain + dot(grad_up, up_w, ((1,), (1,))) * ln2_gain
    )
    grad_unit = own_rows(partial_unit.reshape(*grouped, width))
    centre = own_x - jnp.mean(own_x, -1, keepdims=True)
    scale = lax.rsqrt(jnp.mean(centre * centre, -1, keepdims=True) + norm_eps)
    own_unit = centre * scale
    back = scale * (
        grad_unit
        - jnp.mean(grad_unit, -1, keepdims=True)
        - own_unit * jnp.mean(grad_unit * own_unit, -1, keepdims=True)
    )
    grad_rows = both_cores((own_g + back).astype(low))

    def owned(grad):
        some = lax.psum_scatter(grad.astype(low), "dp", scatter_dimension=0, tiled=True)
        return exchange(some, 0, 1)

    g_down = dot(g_all, acted, ((0,), (0,)))
    g_out = dot(g_all, attended, ((0,), (0,)))
    g_up = dot(normed_two, grad_up, ((0,), (0,)))
    g_qkv = dot(normed_one, grad_qkv, ((0,), (0,)))
    sum_up = jnp.sum(grad_up.astype(full), 0)
    sum_qkv = jnp.sum(grad_qkv.astype(full), 0)
    ln1_shift = jnp.sum(qkv_w.astype(full) * sum_qkv, 1)
    ln2_shift = jnp.sum(up_w.astype(full) * sum_up, 1)
    ln1_scale = (jnp.sum(qkv_w.astype(full) * g_qkv, 1) - ln1_shift * ln1_bias) / ln1_gain
    ln2_scale = (jnp.sum(up_w.astype(full) * g_up, 1) - ln2_shift * ln2_bias) / ln2_gain
    down_part, up_part = owned(g_down), owned(g_up)
    out_part, qkv_part = owned(g_out), owned(g_qkv)

    norms = jnp.concatenate([ln1_scale, ln1_shift, ln2_scale, ln2_shift])
    norms = norms + partner(norms)
    spot = jnp.zeros((3, ctx, heads * head), full)
    spot = lax.dynamic_update_slice_in_dim(spot, sum_qkv.reshape(3, 1, -1), here, 1)
    up_spot = lax.dynamic_update_slice_in_dim(
        jnp.zeros((ctx * hidden,), full), sum_up, here * hidden, 0
    )
    small = jnp.concatenate(
        [norms, jnp.sum(cots.astype(full), (0, 1)), spot.reshape(-1), up_spot]
    )
    for axis, size in (("ctx", ctx), ("dp", reps)):
        step = 1
        while step < size:
            small = small + swap(small, axis, size, step)
            step *= 2
    ends = [width, 2 * width, 3 * width, 4 * width, 5 * width]
    ends.append(ends[-1] + spot.size)
    first, second, third, fourth, cot_sum, spot, up_sum = jnp.split(small, ends)

    near = width // (reps * ctx)
    return (
        out_rows,
        grad_rows,
        first,
        second,
        third,
        fourth,
        jnp.swapaxes(qkv_part.reshape(near, ctx, 3, heads, head), 1, 2)
        .reshape(near, 3, ctx * heads, head)
        .astype(full),
        spot.reshape(3, ctx * heads, head),
        out_part.T.reshape(ctx * heads, head, near).astype(full),
        cot_sum,
        up_part.astype(full),
        up_sum,
        down_part.T.astype(full),
        cot_sum,
    )
def layer_norm(values, gain, shift):
    centre = values - jnp.mean(values, -1, keepdims=True)
    spread = jnp.mean(centre * centre, -1, keepdims=True)
    return centre * lax.rsqrt(spread + norm_eps) * gain + shift


def rotate(values, positions):
    half_rot = ROT // 2
    freqs = jnp.exp(jnp.arange(half_rot, dtype=jnp.float32) * (-2.0 * math.log(10000.0) / ROT))
    angles = positions[:, None].astype(jnp.float32) * freqs[None, :]
    angles = jnp.concatenate([angles, angles], -1)
    cosine = jnp.cos(angles)[:, None, :]
    sine = jnp.sin(angles)[:, None, :]
    rotary = values[..., :ROT]
    turned = jnp.concatenate([-rotary[..., half_rot:], rotary[..., :half_rot]], -1)
    return jnp.concatenate([rotary * cosine + turned * sine, values[..., ROT:]], -1)


def masked_scores(queries, keys_all, score_scale, key_limit):
    scores = (
        jnp.einsum("qhe,khe->hqk", queries, keys_all, preferred_element_type=jnp.float32)
        * score_scale
    )
    allowed = jnp.arange(keys_all.shape[0], dtype=jnp.int32) < key_limit
    return jnp.where(allowed[None, None, :], scores, masked_value)


def gathered_body(
    layer_input,
    out_grad,
    seq_count,
    seq_order,
    ln1_gain,
    ln1_bias,
    ln2_gain,
    ln2_bias,
    w_qkv,
    b_qkv,
    w_out,
    b_out,
    w_up,
    b_up,
    w_down,
    b_down,
):
    full_qkv, full_out, full_up, full_down = (
        lax.all_gather(w_qkv, "ctx", axis=0, tiled=True),
        lax.all_gather(w_out, "ctx", axis=2, tiled=True),
        lax.all_gather(w_up, "ctx", axis=0, tiled=True),
        lax.all_gather(w_down, "ctx", axis=1, tiled=True),
    )
    block_len = layer_input.shape[2]
    slot_total = layer_input.shape[1]
    ctx_index = lax.axis_index("ctx")
    positions = ctx_index * block_len + jnp.arange(block_len, dtype=jnp.int32)
    key_limit = (ctx_index + 1) * block_len
    score_scale = 1.0 / math.sqrt(w_qkv.shape[3])
    zero_index = jnp.int32(0)
    gelu_exact = functools.partial(jax.nn.gelu, approximate=False)
    live_count = seq_count[0]

    def one_sequence(turn, carry):
        out_buf, grad_buf, grads = carry
        slot_id = seq_order[0, turn]
        live_here = (turn < live_count).astype(jnp.float32)
        x_rows = lax.dynamic_index_in_dim(layer_input[0], slot_id, 0, keepdims=False)
        cot_given = lax.dynamic_index_in_dim(out_grad[0], slot_id, 0, keepdims=False)
        x_float = x_rows.astype(jnp.float32)
        cot_float = cot_given.astype(jnp.float32) * live_here
        cot_rows = cot_float.astype(jnp.bfloat16)
        normed_one = layer_norm(x_float, ln1_gain, ln1_bias).astype(jnp.bfloat16)
        normed_two = layer_norm(x_float, ln2_gain, ln2_bias).astype(jnp.bfloat16)
        projected = (
            jnp.einsum("td,dshe->tshe", normed_one, full_qkv, preferred_element_type=jnp.float32)
            + b_qkv
        )
        rot_pull = jax.vjp(lambda values: rotate(values, positions), projected[:, 0])[1]
        queries = rotate(projected[:, 0], positions).astype(jnp.bfloat16)
        keys_own = rotate(projected[:, 1], positions).astype(jnp.bfloat16)
        values_own = projected[:, 2].astype(jnp.bfloat16)
        keys_all, values_all = (
            lax.all_gather(keys_own, "ctx", axis=0, tiled=True),
            lax.all_gather(values_own, "ctx", axis=0, tiled=True),
        )
        masked = masked_scores(queries, keys_all, score_scale, key_limit)
        row_peak = jnp.max(masked, -1, keepdims=True)
        expo = jnp.exp(masked - row_peak)
        row_total = jnp.sum(expo, -1, keepdims=True)
        log_total = row_peak + jnp.log(row_total)
        probs_low = (expo / row_total).astype(jnp.bfloat16)
        attended = jnp.einsum(
            "hqk,khe->qhe", probs_low, values_all, preferred_element_type=jnp.float32
        ).astype(jnp.bfloat16)
        up_pre = jnp.dot(normed_two, full_up, preferred_element_type=jnp.float32) + b_up
        acted = gelu_exact(up_pre).astype(jnp.bfloat16)
        partial_out = jnp.einsum(
            "the,hed->td", attended, full_out, preferred_element_type=jnp.float32
        ) + jnp.dot(acted, full_down, preferred_element_type=jnp.float32)
        branch = lax.psum(partial_out, "tensor")
        out_rows = ((x_float + branch + b_out + b_down) * live_here).astype(jnp.bfloat16)
        grad_attended = jnp.einsum(
            "td,hed->the", cot_rows, full_out, preferred_element_type=jnp.float32
        ).astype(jnp.bfloat16)
        grad_acted = jnp.einsum(
            "td,fd->tf", cot_rows, full_down, preferred_element_type=jnp.float32
        )
        grad_up = jax.vjp(gelu_exact, up_pre)[1](grad_acted)[0].astype(jnp.bfloat16)
        grad_two = jnp.einsum("tf,df->td", grad_up, full_up, preferred_element_type=jnp.float32)
        masked = masked_scores(queries, keys_all, score_scale, key_limit)
        probs = jnp.exp(masked - log_total)
        probs_again = probs.astype(jnp.bfloat16)
        grad_probs = jnp.einsum(
            "qhe,khe->hqk", grad_attended, values_all, preferred_element_type=jnp.float32
        )
        grad_scores = (
            probs * (grad_probs - jnp.sum(probs * grad_probs, -1, keepdims=True))
        ).astype(jnp.bfloat16)
        grad_queries = (
            jnp.einsum("hqk,khe->qhe", grad_scores, keys_all, preferred_element_type=jnp.float32)
            * score_scale
        )
        grad_keys_all = (
            jnp.einsum("hqk,qhe->khe", grad_scores, queries, preferred_element_type=jnp.float32)
            * score_scale
        )
        grad_values_all = jnp.einsum(
            "hqk,qhe->khe", probs_again, grad_attended, preferred_element_type=jnp.float32
        )
        grad_keys, grad_values = (
            lax.psum_scatter(grad_keys_all, "ctx", scatter_dimension=0, tiled=True),
            lax.psum_scatter(grad_values_all, "ctx", scatter_dimension=0, tiled=True),
        )
        grad_proj = jnp.stack(
            [rot_pull(grad_queries)[0], rot_pull(grad_keys)[0], grad_values], axis=1
        ).astype(jnp.bfloat16)
        grad_one = jnp.einsum(
            "tshe,dshe->td", grad_proj, full_qkv, preferred_element_type=jnp.float32
        )
        sum_one, sum_two = lax.psum((grad_one, grad_two), "tensor")
        back_one = jax.vjp(layer_norm, x_float, ln1_gain, ln1_bias)[1](sum_one)
        back_two = jax.vjp(layer_norm, x_float, ln2_gain, ln2_bias)[1](sum_two)
        grad_rows = (cot_float + back_one[0] + back_two[0]).astype(jnp.bfloat16)
        cot_total = jnp.sum(cot_float, 0)
        grads = (
            grads[0]
            + jnp.einsum(
                "td,tshe->dshe", normed_one, grad_proj, preferred_element_type=jnp.float32
            ),
            grads[1]
            + jnp.einsum("the,td->hed", attended, cot_rows, preferred_element_type=jnp.float32),
            grads[2]
            + jnp.einsum("td,tf->df", normed_two, grad_up, preferred_element_type=jnp.float32),
            grads[3] + jnp.einsum("tf,td->fd", acted, cot_rows, preferred_element_type=jnp.float32),
            grads[4] + back_one[1],
            grads[5] + back_one[2],
            grads[6] + back_two[1],
            grads[7] + back_two[2],
            grads[8] + jnp.sum(grad_proj.astype(jnp.float32), 0),
            grads[9] + cot_total,
            grads[10] + jnp.sum(grad_up.astype(jnp.float32), 0),
            grads[11] + cot_total,
        )
        out_buf = lax.dynamic_update_slice(
            out_buf, out_rows[None, None], (zero_index, slot_id, zero_index, zero_index)
        )
        grad_buf = lax.dynamic_update_slice(
            grad_buf, grad_rows[None, None], (zero_index, slot_id, zero_index, zero_index)
        )
        return (out_buf, grad_buf, grads)

    start_grads = (
        jnp.zeros(full_qkv.shape, jnp.float32),
        jnp.zeros(full_out.shape, jnp.float32),
        jnp.zeros(full_up.shape, jnp.float32),
        jnp.zeros(full_down.shape, jnp.float32),
        jnp.zeros_like(ln1_gain),
        jnp.zeros_like(ln1_bias),
        jnp.zeros_like(ln2_gain),
        jnp.zeros_like(ln2_bias),
        jnp.zeros_like(b_qkv),
        jnp.zeros_like(b_out),
        jnp.zeros_like(b_up),
        jnp.zeros_like(b_down),
    )
    start = (
        jnp.zeros(layer_input.shape, jnp.bfloat16),
        jnp.zeros(layer_input.shape, jnp.bfloat16),
        start_grads,
    )
    out_buf, grad_buf, grads = lax.fori_loop(0, slot_total, one_sequence, start)
    reduced = (
        lax.psum_scatter(grads[0], ("dp", "ctx"), scatter_dimension=0, tiled=True),
        lax.psum_scatter(grads[1], ("dp", "ctx"), scatter_dimension=2, tiled=True),
        lax.psum_scatter(grads[2], ("dp", "ctx"), scatter_dimension=0, tiled=True),
        lax.psum_scatter(grads[3], ("dp", "ctx"), scatter_dimension=1, tiled=True),
    )
    small = lax.psum(
        (grads[4], grads[5], grads[6], grads[7], grads[8], grads[9], grads[10], grads[11]),
        ("dp", "ctx"),
    )
    return (
        out_buf,
        grad_buf,
        small[0],
        small[1],
        small[2],
        small[3],
        reduced[0],
        small[4],
        reduced[1],
        small[5],
        reduced[2],
        small[6],
        reduced[3],
        small[7],
    )


def body(*args):
    ctx, cores, reps = lax.axis_size("ctx"), lax.axis_size("tensor"), lax.axis_size("dp")
    _, slots, block_len, width = args[0].shape
    split = (
        ctx == 4
        and cores == 2
        and slots == 2
        and args[8].shape[2] == ctx
        and reps & (reps - 1) == 0
        and block_len % (cores * 16) == 0
        and width % (reps * ctx) == 0
    )
    return (split_body if split else gathered_body)(*args)


def solution(mesh):
    placed = (
        P("dp", None, "ctx", None),
        P("dp", None, "ctx", None),
        P("dp"),
        P("dp", None),
        P(),
        P(),
        P(),
        P(),
        P("ctx", None, "tensor", None),
        P(None, "tensor", None),
        P("tensor", None, "ctx"),
        P(),
        P("ctx", "tensor"),
        P("tensor"),
        P("tensor", "ctx"),
        P(),
    )
    return jax.shard_map(
        body,
        mesh=mesh,
        in_specs=placed,
        out_specs=(
            P("dp", None, "ctx", None),
            P("dp", None, "ctx", None),
            P(),
            P(),
            P(),
            P(),
            P(("dp", "ctx"), None, "tensor", None),
            P(None, "tensor", None),
            P("tensor", None, ("dp", "ctx")),
            P(),
            P(("dp", "ctx"), "tensor"),
            P("tensor"),
            P("tensor", ("dp", "ctx")),
            P(),
        ),
        check_vma=False,
    )
```

```python
import functools
import math

import jax
import jax.numpy as jnp
from jax import lax
from jax.experimental import pallas as pl
from jax.experimental.pallas import tpu as pltpu
from jax.sharding import PartitionSpec as P

ROT = 64


norm_eps = 1e-05
masked_value = -1e30
low = jnp.bfloat16
full = jnp.float32
NN, NT, TN = ((1,), (0,)), ((1,), (1,)), ((0,), (0,))


def swap(value, axis, size, step):
    return lax.ppermute(value, axis, [(i, i ^ step) for i in range(size)])


def after(value, *others):
    return lax.optimization_barrier((value, *others))[0]


def dot(left, right, dims):
    return lax.dot_general(left, right, (dims, ((), ())), preferred_element_type=full)


def rotary_tables(positions, lanes):
    half_rot = ROT // 2
    freqs = jnp.exp(jnp.arange(half_rot, dtype=full) * (-2.0 * math.log(10000.0) / ROT))
    angles = positions[:, None].astype(full) * freqs[None, :]
    cosine, sine = jnp.cos(angles), jnp.sin(angles)
    rest = (positions.shape[0], lanes - ROT)
    return (
        jnp.concatenate([cosine, cosine, jnp.ones(rest, full)], -1),
        jnp.concatenate([-sine, sine, jnp.zeros(rest, full)], -1),
    )


def whole_spec(shape):
    return pl.BlockSpec(tuple(shape), lambda *_: (0,) * len(shape))


def call(kernel, grid, here, inputs, outputs, scratch=(), vmem=56):
    return pl.pallas_call(
        kernel,
        out_shape=tuple(jax.ShapeDtypeStruct(shape, kind) for shape, kind, _ in outputs),
        grid_spec=pltpu.PrefetchScalarGridSpec(
            num_scalar_prefetch=1,
            grid=grid,
            in_specs=[spec for _, spec in inputs],
            out_specs=tuple(spec for _, _, spec in outputs),
            scratch_shapes=list(scratch),
        ),
        compiler_params=pltpu.CompilerParams(vmem_limit_bytes=vmem << 20),
    )(here, *(array for array, _ in inputs))


def lanes_of(here_ref, k, size):
    return pl.ds(pl.multiple_of(jnp.bitwise_xor(here_ref[0], k) * size, size), size)


def gelu_both(values):
    cumulative = 0.5 * (1.0 + lax.erf(values * math.sqrt(0.5)))
    density = jnp.exp(-0.5 * values * values) * (1.0 / math.sqrt(2.0 * math.pi))
    return values * cumulative, cumulative + values * density


def up_kernel(
    here, x_ref, g1, b1, g2, b2, w0, w1, w2, w3, bias, h1_ref, h2_ref, act_ref, slope_ref
):
    values = x_ref[...].astype(full)
    centre = values - jnp.mean(values, -1, keepdims=True)
    spread = jnp.mean(centre * centre, -1, keepdims=True)
    unit = centre * lax.rsqrt(spread + norm_eps)
    h1_ref[...] = (unit * g1[...] + b1[...]).astype(low)
    h2_ref[...] = (unit * g2[...] + b2[...]).astype(low)
    depth, hidden = w1.shape
    step = min(hidden, 256)
    for n in range(hidden // step):
        cols = slice(n * step, (n + 1) * step)
        total = bias[:, cols]
        for k, w in enumerate((w0, w1, w2, w3)):
            total = total + dot(h2_ref[:, lanes_of(here, k, depth)], w[:, cols], NN)
        acted, slope = gelu_both(total)
        act_ref[:, cols] = acted.astype(low)
        slope_ref[:, cols] = slope.astype(slope_ref.dtype)


def up_projection(here, x, gains, pieces, w_up, b_up, tile=256):
    tokens, width = x.shape
    depth, hidden = pieces[0].shape
    tile = min(tile, tokens)
    row = pl.BlockSpec((tile, width), lambda i, c: (i, 0))
    out = pl.BlockSpec((tile, hidden), lambda i, c: (i, 0))
    vector = whole_spec((1, width))
    return call(
        up_kernel,
        (tokens // tile,),
        here,
        [(x, row)]
        + [(gain, vector) for gain in gains]
        + [(w_up, pl.BlockSpec((depth, hidden), lambda i, c: (0, c[0])))]
        + [(piece, whole_spec(piece.shape)) for piece in pieces]
        + [(b_up, pl.BlockSpec((1, hidden), lambda i, c: (0, c[0])))],
        [
            ((tokens, width), low, row),
            ((tokens, width), low, row),
            ((tokens, hidden), low, out),
            ((tokens, hidden), full, out),
        ],
    )


def slope_kernel(here, g_ref, w0, w1, w2, w3, slope_ref, du_ref, sum_ref):
    hidden, depth = w1.shape

    @pl.when(pl.program_id(0) == 0)
    def _():
        sum_ref[...] = jnp.zeros_like(sum_ref)

    step = min(hidden, 256)
    for n in range(hidden // step):
        cols = slice(n * step, (n + 1) * step)
        total = None
        for k, w in enumerate((w0, w1, w2, w3)):
            part = dot(g_ref[:, lanes_of(here, k, depth)], w[cols, :], NT)
            total = part if total is None else total + part
        du = (total * slope_ref[:, cols].astype(full)).astype(low)
        du_ref[:, cols] = du
        sum_ref[:, cols] += jnp.sum(du.astype(full), 0, keepdims=True)


def hidden_grads(here, g, slope, pieces, w_down, tile=256):
    tokens, width = g.shape
    hidden, depth = pieces[0].shape
    tile = min(tile, tokens)
    out = pl.BlockSpec((tile, hidden), lambda i, c: (i, 0))
    return call(
        slope_kernel,
        (tokens // tile,),
        here,
        [(g, pl.BlockSpec((tile, width), lambda i, c: (i, 0)))]
        + [(w_down, pl.BlockSpec((hidden, depth), lambda i, c: (c[0], 0)))]
        + [(piece, whole_spec(piece.shape)) for piece in pieces]
        + [(slope, out)],
        [((tokens, hidden), low, out), ((1, hidden), full, whole_spec((1, hidden)))],
    )


def projection_kernel(here, h_ref, g_ref, w0, w1, w2, w3, bias, qkv_ref, do_ref):
    depth = w1.shape[0]
    wide = bias.shape[-1]
    total, grads = bias[...], None
    for k, w in enumerate((w0, w1, w2, w3)):
        at = lanes_of(here, k, depth)
        total = total + dot(h_ref[:, at], w[:, :wide], NN)
        part = dot(g_ref[:, at], w[:, wide:], NN)
        grads = part if grads is None else grads + part
    qkv_ref[...] = total
    do_ref[...] = grads.astype(low)


def projections(here, h, g, pieces, w_attn, bias, tile=256):
    tokens, width = h.shape
    depth, hidden = pieces[0].shape
    wide = bias.shape[-1]
    tile = min(tile, tokens)
    row = pl.BlockSpec((tile, width), lambda i, c: (i, 0))
    return call(
        projection_kernel,
        (tokens // tile,),
        here,
        [(h, row), (g, row), (w_attn, pl.BlockSpec((depth, hidden), lambda i, c: (0, c[0])))]
        + [(piece, whole_spec(piece.shape)) for piece in pieces]
        + [(bias, whole_spec(bias.shape))],
        [
            ((tokens, wide), full, pl.BlockSpec((tile, wide), lambda i, c: (i, 0))),
            ((tokens, hidden - wide), low, pl.BlockSpec((tile, hidden - wide), lambda i, c: (i, 0))),
        ],
    )


def attention_kernel(
    here,
    qkv_0,
    qkv_1,
    do_0,
    do_1,
    cos_ref,
    sin_ref,
    o_0,
    o_1,
    dqkv_0,
    dqkv_1,
    q_s,
    k_s,
    v_s,
    do_s,
    dk_s,
    dv_s,
):
    blocks, _, rows, width = qkv_0.shape
    pairs = ((qkv_0, do_0, o_0, dqkv_0), (qkv_1, do_1, o_1, dqkv_1))
    head = width // 3
    lanes = cos_ref.shape[-1]
    size = 2 * rows
    lane = lax.broadcasted_iota(jnp.int32, (rows, lanes), 1)
    first = lane < ROT // 2

    def turn(values, cosine, sine):
        part = values[:, :lanes]
        swapped = jnp.where(
            first, pltpu.roll(part, lanes - ROT // 2, 1), pltpu.roll(part, ROT // 2, 1)
        )
        return jnp.concatenate([part * cosine + swapped * sine, values[:, lanes:]], -1)

    dk_s[...] = jnp.zeros_like(dk_s)
    dv_s[...] = jnp.zeros_like(dv_s)
    for block in range(blocks):
        place = jnp.bitwise_xor(here[0], block)
        for part, (qkv_ref, do_ref, _, _) in enumerate(pairs):
            at = slice(block * size + part * rows, block * size + (part + 1) * rows)
            values = qkv_ref[place, 0]
            cosine, sine = cos_ref[part, place], sin_ref[part, place]
            q_s[at, :] = turn(values[:, :head], cosine, sine).astype(low)
            k_s[at, :] = turn(values[:, head : 2 * head], cosine, sine).astype(low)
            v_s[at, :] = values[:, 2 * head :].astype(low)
            do_s[at, :] = do_ref[place, 0]
    scale = 1.0 / math.sqrt(head)
    for block in range(blocks):
        place = jnp.bitwise_xor(here[0], block)
        own = slice(block * size, (block + 1) * size)
        seen = slice(0, (block + 1) * size)
        q, do = q_s[own, :], do_s[own, :]
        k, v = k_s[seen, :], v_s[seen, :]
        scores = dot(q, k, NT) * scale
        expo = jnp.exp(scores - jnp.max(scores, -1, keepdims=True))
        probs = expo / jnp.sum(expo, -1, keepdims=True)
        probs_low = probs.astype(low)
        attended = dot(probs_low, v, NN).astype(low)
        grad_probs = dot(do, v, NT)
        grad_scores = (
            probs * (grad_probs - jnp.sum(probs * grad_probs, -1, keepdims=True))
        ).astype(low)
        dq = dot(grad_scores, k, NN) * scale
        dk_s[seen, :] += dot(grad_scores, q, TN) * scale
        dv_s[seen, :] += dot(probs_low, do, TN)
        for part, (_, _, o_ref, dqkv_ref) in enumerate(pairs):
            at = slice(part * rows, (part + 1) * rows)
            cosine, sine = cos_ref[part, place], sin_ref[part, place]
            o_ref[place, 0] = attended[at]
            dqkv_ref[place, 0, :, :head] = turn(dq[at], cosine, -sine).astype(low)
    for block in range(blocks):
        place = jnp.bitwise_xor(here[0], block)
        for part, (_, _, _, dqkv_ref) in enumerate(pairs):
            at = slice(block * size + part * rows, block * size + (part + 1) * rows)
            cosine, sine = cos_ref[part, place], sin_ref[part, place]
            dqkv_ref[place, 0, :, head : 2 * head] = turn(dk_s[at, :], cosine, -sine).astype(low)
            dqkv_ref[place, 0, :, 2 * head :] = dv_s[at, :].astype(low)


def attention(here, qkv, grad_o, cosine, sine):
    blocks, slots, rows, width = qkv[0].shape
    head = width // 3
    total = 2 * blocks * rows

    def piece(last):
        return pl.BlockSpec((blocks, 1, rows, last), lambda s, c: (0, s, 0, 0))

    table = whole_spec(cosine.shape)
    return call(
        attention_kernel,
        (slots,),
        here,
        [(part, piece(width)) for part in qkv]
        + [(part, piece(head)) for part in grad_o]
        + [(cosine, table), (sine, table)],
        [((blocks, slots, rows, head), low, piece(head))] * 2
        + [((blocks, slots, rows, width), low, piece(width))] * 2,
        [pltpu.VMEM((total, head), low)] * 4 + [pltpu.VMEM((total, head), full)] * 2,
    )


def out_kernel(here, act_ref, o_ref, d0, d1, d2, d3, a0, a1, a2, a3, out_ref):
    depth = d1.shape[1]
    wide = a1.shape[1] - o_ref.shape[1]
    for k, (down, attn) in enumerate(((d0, a0), (d1, a1), (d2, a2), (d3, a3))):
        total = dot(act_ref[...], down[...], NN) + dot(o_ref[...], attn[:, wide:], NT)
        out_ref[:, lanes_of(here, k, depth)] = total.astype(low)


def out_partial(here, acted, attended, down_pieces, w_down, attn_pieces, w_attn, tile=512):
    tokens, hidden = acted.shape
    head = attended.shape[1]
    depth = down_pieces[0].shape[1]
    width = depth * (1 + len(down_pieces))
    tile = min(tile, tokens)
    return call(
        out_kernel,
        (tokens // tile,),
        here,
        [
            (acted, pl.BlockSpec((tile, hidden), lambda i, c: (i, 0))),
            (attended, pl.BlockSpec((tile, head), lambda i, c: (i, 0))),
            (w_down, pl.BlockSpec((hidden, depth), lambda i, c: (c[0], 0))),
        ]
        + [(piece, whole_spec(piece.shape)) for piece in down_pieces]
        + [(w_attn, pl.BlockSpec(attn_pieces[0].shape, lambda i, c: (0, c[0])))]
        + [(piece, whole_spec(piece.shape)) for piece in attn_pieces],
        [((tokens, width), low, pl.BlockSpec((tile, width), lambda i, c: (i, 0)))],
    )[0]


def unit_kernel(here, dqkv_ref, du_ref, a0, a1, a2, a3, u0, u1, u2, u3, g1, g2, out_ref):
    depth = u1.shape[0]
    wide = dqkv_ref.shape[1]
    for k, (attn, up) in enumerate(((a0, u0), (a1, u1), (a2, u2), (a3, u3))):
        at = lanes_of(here, k, depth)
        total = dot(dqkv_ref[...], attn[:, :wide], NT) * g1[:, at]
        total = total + dot(du_ref[...], up[...], NT) * g2[:, at]
        out_ref[:, at] = total.astype(low)


def unit_partial(here, dqkv, du, attn_pieces, w_attn, up_pieces, w_up, g1, g2, tile=512):
    tokens, hidden = du.shape
    wide = dqkv.shape[1]
    depth = up_pieces[0].shape[0]
    width = g1.shape[1]
    tile = min(tile, tokens)
    first = pl.BlockSpec((depth, hidden), lambda i, c: (0, c[0]))
    return call(
        unit_kernel,
        (tokens // tile,),
        here,
        [
            (dqkv, pl.BlockSpec((tile, wide), lambda i, c: (i, 0))),
            (du, pl.BlockSpec((tile, hidden), lambda i, c: (i, 0))),
            (w_attn, first),
        ]
        + [(piece, whole_spec(piece.shape)) for piece in attn_pieces]
        + [(w_up, first)]
        + [(piece, whole_spec(piece.shape)) for piece in up_pieces]
        + [(g1, whole_spec(g1.shape)), (g2, whole_spec(g2.shape))],
        [((tokens, width), low, pl.BlockSpec((tile, width), lambda i, c: (i, 0)))],
    )[0]


def plain_grad_kernel(here, l_0, l_1, r_0, r_1, out_ref):
    out_ref[...] = (dot(l_0[...], r_0[...], TN) + dot(l_1[...], r_1[...], TN)).astype(low)


def plain_grad(here, left, right, tile=512):
    tokens, width = left[0].shape
    cols = right[0].shape[1]
    tile = min(tile, width)
    return call(
        plain_grad_kernel,
        (width // tile,),
        here,
        [(part, pl.BlockSpec((tokens, tile), lambda i, c: (0, i))) for part in left]
        + [(part, whole_spec(part.shape)) for part in right],
        [((width, cols), low, pl.BlockSpec((tile, cols), lambda i, c: (i, 0)))],
    )[0]


def norm_sums(stats_ref, weights, grads, sums):
    weights = weights.astype(full)
    stats_ref[:, 0:1] = jnp.sum(weights * grads, 1, keepdims=True)
    stats_ref[:, 1:2] = jnp.sum(weights * sums, 1, keepdims=True)


def up_grad_kernel(here, l_0, l_1, r_0, r_1, w0, w1, w2, w3, sums, out_ref, stats_ref):
    grads = dot(l_0[...], r_0[...], TN) + dot(l_1[...], r_1[...], TN)
    out_ref[...] = grads.astype(low)
    for k, w in enumerate((w0, w1, w2, w3)):

        @pl.when(pl.program_id(0) == k)
        def _(w=w):
            norm_sums(stats_ref, w[...], grads, sums[...])


def up_grad(here, left, right, pieces, w_up, sums):
    tokens, width = left[0].shape
    depth, cols = pieces[0].shape
    return call(
        up_grad_kernel,
        (width // depth,),
        here,
        [(part, pl.BlockSpec((tokens, depth), lambda i, c: (0, i ^ c[0]))) for part in left]
        + [(part, whole_spec(part.shape)) for part in right]
        + [(w_up, pl.BlockSpec((depth, cols), lambda i, c: (0, c[0])))]
        + [(piece, whole_spec(piece.shape)) for piece in pieces]
        + [(sums, whole_spec(sums.shape))],
        [
            ((width, cols), low, pl.BlockSpec((depth, cols), lambda i, c: (i ^ c[0], 0))),
            ((width, 128), full, pl.BlockSpec((depth, 128), lambda i, c: (i ^ c[0], 0))),
        ],
    )


def attn_grad_kernel(
    here, h_0, h_1, d_0, d_1, g_0, g_1, o_0, o_1, w0, w1, w2, w3, out_ref, stats_ref, sum_ref
):
    wide = d_0.shape[1]

    @pl.when(pl.program_id(0) == 0)
    def _():
        sum_ref[...] = jnp.sum(d_0[...].astype(full), 0, keepdims=True) + jnp.sum(
            d_1[...].astype(full), 0, keepdims=True
        )

    grads = dot(h_0[...], d_0[...], TN) + dot(h_1[...], d_1[...], TN)
    out_ref[:, :wide] = grads.astype(low)
    out_ref[:, wide:] = (dot(g_0[...], o_0[...], TN) + dot(g_1[...], o_1[...], TN)).astype(low)
    for k, w in enumerate((w0, w1, w2, w3)):

        @pl.when(pl.program_id(0) == k)
        def _(w=w):
            norm_sums(stats_ref, w[:, :wide], grads, sum_ref[...])


def attn_grad(here, h, dqkv, g, attended, pieces, w_attn):
    tokens, width = h[0].shape
    depth, cols = pieces[0].shape
    wide = dqkv[0].shape[1]
    column = pl.BlockSpec((tokens, depth), lambda i, c: (0, i ^ c[0]))
    return call(
        attn_grad_kernel,
        (width // depth,),
        here,
        [(part, column) for part in h]
        + [(part, whole_spec(part.shape)) for part in dqkv]
        + [(part, column) for part in g]
        + [(part, whole_spec(part.shape)) for part in attended]
        + [(w_attn, pl.BlockSpec((depth, cols), lambda i, c: (0, c[0])))]
        + [(piece, whole_spec(piece.shape)) for piece in pieces],
        [
            ((width, cols), low, pl.BlockSpec((depth, cols), lambda i, c: (i ^ c[0], 0))),
            ((width, 128), full, pl.BlockSpec((depth, 128), lambda i, c: (i ^ c[0], 0))),
            ((1, wide), full, whole_spec((1, wide))),
        ],
    )


def place_rows_kernel(here, p0, p1, p2, p3, out_ref):
    cols = p1.shape[1]
    for k, piece in enumerate((p0, p1, p2, p3)):
        out_ref[:, lanes_of(here, k, cols)] = piece[...].astype(full)


def place_turned_kernel(here, p0, p1, p2, p3, out_ref):
    cols = p1.shape[1]
    for k, piece in enumerate((p0, p1, p2, p3)):
        out_ref[lanes_of(here, k, cols), :] = piece[...].astype(full).T


def place_attn_kernel(here, p0, p1, p2, p3, qkv_ref, out_ref):
    head, _ = out_ref.shape[1:]
    wide = 4 * head
    for k, piece in enumerate((p0, p1, p2, p3)):
        place = jnp.bitwise_xor(here[0], k)
        for i in range(3):
            at = pl.ds(pl.multiple_of(i * wide + place * head, head), head)
            qkv_ref[:, at] = piece[:, i * head : (i + 1) * head].astype(full)
        out_ref[place] = piece[:, 3 * head :].astype(full).T


def placed(kernel, here, chunk, pieces, shapes):
    near, cols = pieces[0].shape
    return call(
        kernel,
        (1,),
        here,
        [(chunk, pl.BlockSpec((near, cols), lambda i, c: (c[0], 0)))]
        + [(piece, whole_spec(piece.shape)) for piece in pieces],
        [(shape, full, whole_spec(shape)) for shape in shapes],
    )


def split_body(
    layer_input,
    out_grad,
    seq_count,
    seq_order,
    ln1_gain,
    ln1_bias,
    ln2_gain,
    ln2_bias,
    w_qkv,
    b_qkv,
    w_out,
    b_out,
    w_up,
    b_up,
    w_down,
    b_down,
):
    ctx, cores, reps = lax.axis_size("ctx"), lax.axis_size("tensor"), lax.axis_size("dp")
    _, slots, block_len, width = layer_input.shape
    index, core = lax.axis_index("ctx"), lax.axis_index("tensor")
    here = index[None].astype(jnp.int32)
    rows = block_len // cores
    head = w_qkv.shape[3]
    hidden = w_up.shape[1] // ctx
    depth = width // ctx
    near = depth // reps
    grouped = (ctx, slots, rows)

    def across(value, step):
        return swap(value, "ctx", ctx, step)

    def partner(value):
        return swap(value, "tensor", cores, 1)

    def slices(value, each, axis):
        return [
            lax.dynamic_slice_in_dim(value, (index ^ k) * each, each, axis) for k in range(1, ctx)
        ]

    def sends(parts):
        return [across(part, k + 1) for k, part in enumerate(parts)]

    def own_part(value):
        return lax.dynamic_slice_in_dim(value, core * rows, rows, 1)

    def gather(own):
        first, second = across(own, 1), across(own, 2)
        third = across(first[:1], 2)
        fourth = across(second[1:], 1)
        third = jnp.concatenate([third, fourth], 0)
        return jnp.stack([own, first, second, third]), (first, second, third)

    def reduced(mine, theirs):
        mine = mine.reshape(*grouped, width)
        other = partner(theirs).reshape(*grouped, width)

        def both(k, slot):
            return mine[k, slot].astype(full) + other[k, slot].astype(full)

        every, head_slot, tail = slice(None), slice(0, 1), slice(1, None)
        by_two = across(both(3, head_slot).astype(low), 2)
        by_one = across(both(3, tail).astype(low), 1)
        first = jnp.concatenate([both(1, head_slot) + by_two.astype(full), both(1, tail)], 0)
        second = jnp.concatenate([both(2, head_slot), both(2, tail) + by_one.astype(full)], 0)
        first = across(first.astype(low), 1)
        second = across(second.astype(low), 2)
        return both(0, every) + first.astype(full) + second.astype(full)

    def both_cores(mine):
        theirs = partner(mine)
        low_rows = jnp.where(core == 0, mine, theirs)
        high_rows = jnp.where(core == 0, theirs, mine)
        return jnp.concatenate([low_rows, high_rows], 1)[None]

    turns = jnp.arange(slots, dtype=jnp.int32)
    taken = (seq_order[0][:, None] == turns[None, :]) & (turns[:, None] < seq_count[0])
    live = jnp.any(taken, axis=0).astype(full)[:, None, None]
    inputs = layer_input[0]
    cots = (out_grad[0].astype(full) * live).astype(low)

    heads = w_qkv.shape[2]
    w_attn = jnp.concatenate(
        [
            jnp.swapaxes(w_qkv, 1, 2).reshape(depth, heads, 3 * head),
            w_out.reshape(heads * head, depth).T.reshape(depth, heads, head),
        ],
        -1,
    ).reshape(depth, heads * 4 * head)
    parity = lax.axis_index("dp") % 2
    half = hidden // 2
    up_pieces = []
    for k in range(1, ctx):
        at = (index ^ k) * hidden + parity * half
        one = across(lax.dynamic_slice_in_dim(w_up, at, half, 1), k)
        two = swap(one, "dp", reps, 1)
        up_pieces.append(
            jnp.where(
                parity == 0, jnp.concatenate([one, two], 1), jnp.concatenate([two, one], 1)
            )
        )
    down_slices = slices(w_down, hidden, 0)
    attn_slices = slices(w_attn, hidden, 1)
    down_pieces = sends(down_slices)
    attn_pieces = sends(attn_slices)
    x_mine = gather(own_part(inputs))[0]
    x_mine = after(x_mine, *down_slices, *attn_slices)
    g_mine, g_pieces = gather(own_part(cots))
    other = lax.dynamic_slice_in_dim(cots, (1 - core) * rows, rows, 1)
    g_other = jnp.stack([other] + [partner(g) for g in g_pieces])

    x_parts = [part.reshape(-1, width) for part in (x_mine, partner(x_mine))]
    g_parts = [part.reshape(-1, width) for part in (g_mine, g_other)]
    gains = [gain[None] for gain in (ln1_gain, ln1_bias, ln2_gain, ln2_bias)]

    ups = []
    for x in x_parts:
        ups.append(up_projection(here, x, gains, up_pieces, w_up, b_up[None]))
    normed_one, normed_two, acted, slopes = zip(*ups)

    def owned(grad):
        return lax.psum_scatter(grad, "dp", scatter_dimension=0, tiled=True)

    down_chunk = plain_grad(here, g_parts, acted)
    down_chunk = owned(down_chunk)
    hiddens = []
    for i in range(cores):
        hiddens.append(hidden_grads(here, g_parts[i], slopes[i], down_pieces, w_down))
    grad_up = [part for part, _ in hiddens]
    sum_up = hiddens[0][1] + hiddens[1][1]
    up_chunk, up_stats = up_grad(here, normed_two, grad_up, up_pieces, w_up, sum_up)
    up_chunk = owned(up_chunk)

    qkv_bias = lax.dynamic_slice_in_dim(b_qkv, index, 1, 1).reshape(1, 3 * head)
    projected = []
    for i in range(cores):
        projected.append(
            projections(here, normed_one[i], g_parts[i], attn_pieces, w_attn, qkv_bias)
        )
    order = jnp.arange(cores * ctx * rows, dtype=jnp.int32)
    part, block, row = order // (ctx * rows), order // rows % ctx, order % rows
    positions = (index ^ block) * block_len + (part ^ core) * rows + row
    lanes = min(head, 128)
    cosine, sine = (
        table.reshape(cores, ctx, rows, lanes) for table in rotary_tables(positions, lanes)
    )
    attended_0, attended_1, dqkv_0, dqkv_1 = attention(
        here,
        [qkv.reshape(*grouped, 3 * head) for qkv, _ in projected],
        [grad_o.reshape(*grouped, head) for _, grad_o in projected],
        cosine,
        sine,
    )
    attended = [part.reshape(-1, head) for part in (attended_0, attended_1)]
    grad_qkv = [part.reshape(-1, 3 * head) for part in (dqkv_0, dqkv_1)]
    attn_chunk, attn_stats, sum_qkv = attn_grad(
        here, normed_one, grad_qkv, g_parts, attended, attn_pieces, w_attn
    )
    attn_chunk = owned(attn_chunk)

    partial_out = []
    for i in range(cores):
        partial_out.append(
            out_partial(
                here, acted[i], attended[i], down_pieces, w_down, attn_pieces, w_attn
            )
        )
    branch = reduced(*partial_out)
    own_x = own_part(inputs).astype(full)
    own_g = own_part(cots).astype(full)
    out_rows = both_cores(((own_x + branch + b_out + b_down) * live).astype(low))

    partial_unit = []
    for i in range(cores):
        partial_unit.append(
            unit_partial(
                here,
                grad_qkv[i],
                grad_up[i],
                attn_pieces,
                w_attn,
                up_pieces,
                w_up,
                ln1_gain[None],
                ln2_gain[None],
            )
        )
    grad_unit = reduced(*partial_unit)
    centre = own_x - jnp.mean(own_x, -1, keepdims=True)
    scale = lax.rsqrt(jnp.mean(centre * centre, -1, keepdims=True) + norm_eps)
    own_unit = centre * scale
    back = scale * (
        grad_unit
        - jnp.mean(grad_unit, -1, keepdims=True)
        - own_unit * jnp.mean(grad_unit * own_unit, -1, keepdims=True)
    )
    grad_rows = both_cores((own_g + back).astype(low))

    ln1_shift, ln2_shift = attn_stats[:, 1], up_stats[:, 1]
    ln1_scale = (attn_stats[:, 0] - ln1_shift * ln1_bias) / ln1_gain
    ln2_scale = (up_stats[:, 0] - ln2_shift * ln2_bias) / ln2_gain
    norms = jnp.concatenate([ln1_scale, ln1_shift, ln2_scale, ln2_shift])
    norms = norms + partner(norms)
    spot = jnp.zeros((3, ctx, head), full)
    spot = lax.dynamic_update_slice_in_dim(spot, sum_qkv.reshape(3, 1, head), index, 1)
    up_spot = lax.dynamic_update_slice_in_dim(
        jnp.zeros((ctx * hidden,), full), sum_up[0], index * hidden, 0
    )
    small = jnp.concatenate(
        [norms, jnp.sum(cots.astype(full), (0, 1)), spot.reshape(-1), up_spot]
    )
    for axis, size in (("ctx", ctx), ("dp", reps)):
        step = 1
        while step < size:
            small = small + swap(small, axis, size, step)
            step *= 2
    ends = [width, 2 * width, 3 * width, 4 * width, 5 * width]
    ends.append(ends[-1] + spot.size)
    first, second, third, fourth, cot_sum, spot, up_sum = jnp.split(small, ends)

    def placing(kernel, chunk, shapes):
        pieces = sends(slices(chunk, near, 0))
        return placed(kernel, here, chunk, pieces, shapes)

    down_grad = placing(place_turned_kernel, down_chunk, [(ctx * hidden, near)])[0]
    up_rows = placing(place_rows_kernel, up_chunk, [(near, ctx * hidden)])[0]
    qkv_rows, out_grads = placing(
        place_attn_kernel, attn_chunk, [(near, 3 * heads * head), (heads, head, near)]
    )
    return (
        out_rows,
        grad_rows,
        first,
        second,
        third,
        fourth,
        qkv_rows.reshape(near, 3, heads, head),
        spot.reshape(3, heads, head),
        out_grads,
        cot_sum,
        up_rows,
        up_sum,
        down_grad,
        cot_sum,
    )


def layer_norm(values, gain, shift):
    centre = values - jnp.mean(values, -1, keepdims=True)
    spread = jnp.mean(centre * centre, -1, keepdims=True)
    return centre * lax.rsqrt(spread + norm_eps) * gain + shift


def rotate(values, positions):
    half_rot = ROT // 2
    freqs = jnp.exp(jnp.arange(half_rot, dtype=jnp.float32) * (-2.0 * math.log(10000.0) / ROT))
    angles = positions[:, None].astype(jnp.float32) * freqs[None, :]
    angles = jnp.concatenate([angles, angles], -1)
    cosine = jnp.cos(angles)[:, None, :]
    sine = jnp.sin(angles)[:, None, :]
    rotary = values[..., :ROT]
    turned = jnp.concatenate([-rotary[..., half_rot:], rotary[..., :half_rot]], -1)
    return jnp.concatenate([rotary * cosine + turned * sine, values[..., ROT:]], -1)


def masked_scores(queries, keys_all, score_scale, key_limit):
    scores = (
        jnp.einsum("qhe,khe->hqk", queries, keys_all, preferred_element_type=jnp.float32)
        * score_scale
    )
    allowed = jnp.arange(keys_all.shape[0], dtype=jnp.int32) < key_limit
    return jnp.where(allowed[None, None, :], scores, masked_value)


def gathered_body(
    layer_input,
    out_grad,
    seq_count,
    seq_order,
    ln1_gain,
    ln1_bias,
    ln2_gain,
    ln2_bias,
    w_qkv,
    b_qkv,
    w_out,
    b_out,
    w_up,
    b_up,
    w_down,
    b_down,
):
    full_qkv, full_out, full_up, full_down = (
        lax.all_gather(w_qkv, "ctx", axis=0, tiled=True),
        lax.all_gather(w_out, "ctx", axis=2, tiled=True),
        lax.all_gather(w_up, "ctx", axis=0, tiled=True),
        lax.all_gather(w_down, "ctx", axis=1, tiled=True),
    )
    block_len = layer_input.shape[2]
    slot_total = layer_input.shape[1]
    ctx_index = lax.axis_index("ctx")
    positions = ctx_index * block_len + jnp.arange(block_len, dtype=jnp.int32)
    key_limit = (ctx_index + 1) * block_len
    score_scale = 1.0 / math.sqrt(w_qkv.shape[3])
    zero_index = jnp.int32(0)
    gelu_exact = functools.partial(jax.nn.gelu, approximate=False)
    live_count = seq_count[0]

    def one_sequence(turn, carry):
        out_buf, grad_buf, grads = carry
        slot_id = seq_order[0, turn]
        live_here = (turn < live_count).astype(jnp.float32)
        x_rows = lax.dynamic_index_in_dim(layer_input[0], slot_id, 0, keepdims=False)
        cot_given = lax.dynamic_index_in_dim(out_grad[0], slot_id, 0, keepdims=False)
        x_float = x_rows.astype(jnp.float32)
        cot_float = cot_given.astype(jnp.float32) * live_here
        cot_rows = cot_float.astype(jnp.bfloat16)
        normed_one = layer_norm(x_float, ln1_gain, ln1_bias).astype(jnp.bfloat16)
        normed_two = layer_norm(x_float, ln2_gain, ln2_bias).astype(jnp.bfloat16)
        projected = (
            jnp.einsum("td,dshe->tshe", normed_one, full_qkv, preferred_element_type=jnp.float32)
            + b_qkv
        )
        rot_pull = jax.vjp(lambda values: rotate(values, positions), projected[:, 0])[1]
        queries = rotate(projected[:, 0], positions).astype(jnp.bfloat16)
        keys_own = rotate(projected[:, 1], positions).astype(jnp.bfloat16)
        values_own = projected[:, 2].astype(jnp.bfloat16)
        keys_all, values_all = (
            lax.all_gather(keys_own, "ctx", axis=0, tiled=True),
            lax.all_gather(values_own, "ctx", axis=0, tiled=True),
        )
        masked = masked_scores(queries, keys_all, score_scale, key_limit)
        row_peak = jnp.max(masked, -1, keepdims=True)
        expo = jnp.exp(masked - row_peak)
        row_total = jnp.sum(expo, -1, keepdims=True)
        log_total = row_peak + jnp.log(row_total)
        probs_low = (expo / row_total).astype(jnp.bfloat16)
        attended = jnp.einsum(
            "hqk,khe->qhe", probs_low, values_all, preferred_element_type=jnp.float32
        ).astype(jnp.bfloat16)
        up_pre = jnp.dot(normed_two, full_up, preferred_element_type=jnp.float32) + b_up
        acted = gelu_exact(up_pre).astype(jnp.bfloat16)
        partial_out = jnp.einsum(
            "the,hed->td", attended, full_out, preferred_element_type=jnp.float32
        ) + jnp.dot(acted, full_down, preferred_element_type=jnp.float32)
        branch = lax.psum(partial_out, "tensor")
        out_rows = ((x_float + branch + b_out + b_down) * live_here).astype(jnp.bfloat16)
        grad_attended = jnp.einsum(
            "td,hed->the", cot_rows, full_out, preferred_element_type=jnp.float32
        ).astype(jnp.bfloat16)
        grad_acted = jnp.einsum(
            "td,fd->tf", cot_rows, full_down, preferred_element_type=jnp.float32
        )
        grad_up = jax.vjp(gelu_exact, up_pre)[1](grad_acted)[0].astype(jnp.bfloat16)
        grad_two = jnp.einsum("tf,df->td", grad_up, full_up, preferred_element_type=jnp.float32)
        masked = masked_scores(queries, keys_all, score_scale, key_limit)
        probs = jnp.exp(masked - log_total)
        probs_again = probs.astype(jnp.bfloat16)
        grad_probs = jnp.einsum(
            "qhe,khe->hqk", grad_attended, values_all, preferred_element_type=jnp.float32
        )
        grad_scores = (
            probs * (grad_probs - jnp.sum(probs * grad_probs, -1, keepdims=True))
        ).astype(jnp.bfloat16)
        grad_queries = (
            jnp.einsum("hqk,khe->qhe", grad_scores, keys_all, preferred_element_type=jnp.float32)
            * score_scale
        )
        grad_keys_all = (
            jnp.einsum("hqk,qhe->khe", grad_scores, queries, preferred_element_type=jnp.float32)
            * score_scale
        )
        grad_values_all = jnp.einsum(
            "hqk,qhe->khe", probs_again, grad_attended, preferred_element_type=jnp.float32
        )
        grad_keys, grad_values = (
            lax.psum_scatter(grad_keys_all, "ctx", scatter_dimension=0, tiled=True),
            lax.psum_scatter(grad_values_all, "ctx", scatter_dimension=0, tiled=True),
        )
        grad_proj = jnp.stack(
            [rot_pull(grad_queries)[0], rot_pull(grad_keys)[0], grad_values], axis=1
        ).astype(jnp.bfloat16)
        grad_one = jnp.einsum(
            "tshe,dshe->td", grad_proj, full_qkv, preferred_element_type=jnp.float32
        )
        sum_one, sum_two = lax.psum((grad_one, grad_two), "tensor")
        back_one = jax.vjp(layer_norm, x_float, ln1_gain, ln1_bias)[1](sum_one)
        back_two = jax.vjp(layer_norm, x_float, ln2_gain, ln2_bias)[1](sum_two)
        grad_rows = (cot_float + back_one[0] + back_two[0]).astype(jnp.bfloat16)
        cot_total = jnp.sum(cot_float, 0)
        grads = (
            grads[0]
            + jnp.einsum(
                "td,tshe->dshe", normed_one, grad_proj, preferred_element_type=jnp.float32
            ),
            grads[1]
            + jnp.einsum("the,td->hed", attended, cot_rows, preferred_element_type=jnp.float32),
            grads[2]
            + jnp.einsum("td,tf->df", normed_two, grad_up, preferred_element_type=jnp.float32),
            grads[3] + jnp.einsum("tf,td->fd", acted, cot_rows, preferred_element_type=jnp.float32),
            grads[4] + back_one[1],
            grads[5] + back_one[2],
            grads[6] + back_two[1],
            grads[7] + back_two[2],
            grads[8] + jnp.sum(grad_proj.astype(jnp.float32), 0),
            grads[9] + cot_total,
            grads[10] + jnp.sum(grad_up.astype(jnp.float32), 0),
            grads[11] + cot_total,
        )
        out_buf = lax.dynamic_update_slice(
            out_buf, out_rows[None, None], (zero_index, slot_id, zero_index, zero_index)
        )
        grad_buf = lax.dynamic_update_slice(
            grad_buf, grad_rows[None, None], (zero_index, slot_id, zero_index, zero_index)
        )
        return (out_buf, grad_buf, grads)

    start_grads = (
        jnp.zeros(full_qkv.shape, jnp.float32),
        jnp.zeros(full_out.shape, jnp.float32),
        jnp.zeros(full_up.shape, jnp.float32),
        jnp.zeros(full_down.shape, jnp.float32),
        jnp.zeros_like(ln1_gain),
        jnp.zeros_like(ln1_bias),
        jnp.zeros_like(ln2_gain),
        jnp.zeros_like(ln2_bias),
        jnp.zeros_like(b_qkv),
        jnp.zeros_like(b_out),
        jnp.zeros_like(b_up),
        jnp.zeros_like(b_down),
    )
    start = (
        jnp.zeros(layer_input.shape, jnp.bfloat16),
        jnp.zeros(layer_input.shape, jnp.bfloat16),
        start_grads,
    )
    out_buf, grad_buf, grads = lax.fori_loop(0, slot_total, one_sequence, start)
    reduced = (
        lax.psum_scatter(grads[0], ("dp", "ctx"), scatter_dimension=0, tiled=True),
        lax.psum_scatter(grads[1], ("dp", "ctx"), scatter_dimension=2, tiled=True),
        lax.psum_scatter(grads[2], ("dp", "ctx"), scatter_dimension=0, tiled=True),
        lax.psum_scatter(grads[3], ("dp", "ctx"), scatter_dimension=1, tiled=True),
    )
    small = lax.psum(
        (grads[4], grads[5], grads[6], grads[7], grads[8], grads[9], grads[10], grads[11]),
        ("dp", "ctx"),
    )
    return (
        out_buf,
        grad_buf,
        small[0],
        small[1],
        small[2],
        small[3],
        reduced[0],
        small[4],
        reduced[1],
        small[5],
        reduced[2],
        small[6],
        reduced[3],
        small[7],
    )


def body(*args):
    ctx, cores, reps = lax.axis_size("ctx"), lax.axis_size("tensor"), lax.axis_size("dp")
    _, slots, block_len, width = args[0].shape
    split = (
        ctx == 4
        and cores == 2
        and slots == 2
        and args[8].shape[2] == ctx
        and args[8].shape[3] % 128 == 0
        and args[12].shape[1] == 4 * ctx * args[8].shape[3]
        and reps > 1
        and reps & (reps - 1) == 0
        and block_len % (cores * 16) == 0
        and width % (reps * ctx * 128) == 0
    )
    if not split:
        return gathered_body(*args)
    return split_body(*args)


def solution(mesh):
    placed = (
        P("dp", None, "ctx", None),
        P("dp", None, "ctx", None),
        P("dp"),
        P("dp", None),
        P(),
        P(),
        P(),
        P(),
        P("ctx", None, "tensor", None),
        P(None, "tensor", None),
        P("tensor", None, "ctx"),
        P(),
        P("ctx", "tensor"),
        P("tensor"),
        P("tensor", "ctx"),
        P(),
    )
    return jax.shard_map(
        body,
        mesh=mesh,
        in_specs=placed,
        out_specs=(
            P("dp", None, "ctx", None),
            P("dp", None, "ctx", None),
            P(),
            P(),
            P(),
            P(),
            P(("dp", "ctx"), None, "tensor", None),
            P(None, "tensor", None),
            P("tensor", None, ("dp", "ctx")),
            P(),
            P(("dp", "ctx"), "tensor"),
            P("tensor"),
            P("tensor", ("dp", "ctx")),
            P(),
        ),
        check_vma=False,
    )
```
